32 devices in a mesh: grp: 4 (over z), tile: 8 (over y, x, core).
Axes of the slice: x: 2, y: 2, z: 4, core: 2. Of those that a mesh axis runs over, the one named last changes fastest.
Arguments:
- right_side: float32 [16, 32768], P(None, ('grp', 'tile')), may hold values from -6 to 6
- ridge: float32 [32768], P(('grp', 'tile')), may hold values from 1 to 4
- tiles: float32 [128, 1024, 1024], P(('grp', 'tile')), may hold values from -0.013671875 to 0.013671875
- tile_list: int32 [128, 2], P(('grp', 'tile')), may hold values from 0 to 31, as said below
Outputs:
- solution: float32 [16, 32768], P(None, ('grp', 'tile'))
- residual: float32 [16, 32768], P(None, ('grp', 'tile'))
The draws below stay inside these ranges and needn't reach their ends.
Inputs may be any that keep to these rules, and one draw needn't show every extreme that they name: `tile_list`: each row is a pair (row block, column block) with row block >= column block; no pair appears twice; rows stand in packed row-major order (row block rising, then column block rising).
All inputs are finite; a program needn't handle non-finite values.
Results may differ from the reference program's by a relative error of at most 0.0003.
Values sent between devices are 32-bit elements; how exact they have to be, the bound alone decides.
A program may use at most 64 MiB of HBM per device.

```python
import math
import jax
import jax.numpy as jnp
from jax import lax

B = 1024
NB = 32
S = 16
ITERS = 2
NP = 32768
NT = 128


def draw_tile_list(key, part):
    total = NB * (NB + 1) // 2
    shuffled = jax.random.permutation(jax.random.fold_in(key, 17), total).astype(jnp.int32)
    dropped = shuffled[:total - NT]
    keep = jnp.ones((total,), jnp.int32).at[dropped].set(0)
    order = jnp.nonzero(keep, size=NT)[0].astype(jnp.int32)
    blocks = jnp.arange(NB, dtype=jnp.int32)
    starts = blocks * (blocks + 1) // 2
    row_block = jnp.sum((starts[None, :] <= order[:, None]).astype(jnp.int32), axis=1) - 1
    row_start = jnp.sum(jnp.where(blocks[None, :] == row_block[:, None], starts[None, :], 0), axis=1)
    col_block = order - row_start
    return jnp.stack([row_block, col_block], axis=1).astype(jnp.int32)


def shard_levels(stream_key, extent, pieces, low, top_value):
    level = 1.0
    for position, parts in pieces:
        draws = jax.random.uniform(jax.random.fold_in(jax.random.fold_in(stream_key, 6), position), (parts,), jnp.float32, low / len(pieces), top_value / len(pieces))
        level = level * jnp.repeat(jnp.exp(draws), extent[position] // parts).reshape((-1,) + (1,) * (len(extent) - 1 - position))
    return level


def bell_draw(rng, extent, spread, most, pieces=(), held_as=jnp.bfloat16):
    result = spread * jax.random.normal(rng, extent, jnp.float32)
    if pieces:
        result = result * shard_levels(rng, extent, pieces, -0.22, 0.18)
    return jnp.clip(result, -most, most).astype(held_as)


def setup_inputs(seed: int = 0) -> dict:
    splits = jax.random.split(jax.random.key(seed), 5)
    right_side = bell_draw(splits[0], (S, NP), 1.0, 6.0, ((1, 32),), jnp.float32)
    ridge = jnp.clip(jnp.exp(math.log(4.0) - 1.3862944 * jax.random.uniform(splits[1], (NP,), jnp.float32) ** shard_levels(splits[1], (NP,), ((0, 32),), -0.2, 0.2)), 1.0, 4.0)
    tiles = bell_draw(splits[2], (NT, B, B), (6 * NB * B) ** -0.5, 0.013671875, ((0, 32),), jnp.float32)
    tile_list = draw_tile_list(jax.random.fold_in(splits[4], 71), 0)
    return dict(right_side=right_side, ridge=ridge, tiles=tiles, tile_list=tile_list)


def gauss_solve(matrix, rhs):
    order = matrix.shape[0]
    for pivot in range(order):
        scale = 1.0 / matrix[pivot, pivot]
        row_new = matrix[pivot] * scale
        rhs_new = rhs[pivot] * scale
        factor = matrix[:, pivot] * (1.0 - (jnp.arange(order) == pivot).astype(matrix.dtype))
        matrix = matrix - factor[:, None] * row_new[None, :]
        rhs = rhs - factor[:, None] * rhs_new[None, :]
        matrix = matrix.at[pivot].set(row_new)
        rhs = rhs.at[pivot].set(rhs_new)
    return rhs


def gram(left, right):
    return lax.dot_general(left, right, (((1,), (1,)), ((), ())), precision=lax.Precision.HIGHEST, preferred_element_type=jnp.float32)


def apply_kernel(tiles, tile_list, field):
    order = tiles.shape[1]
    rowid = lax.broadcasted_iota(jnp.int32, (order, order), 0)
    colid = lax.broadcasted_iota(jnp.int32, (order, order), 1)
    lower = rowid >= colid
    strict = rowid > colid

    def step(total, item):
        tile, pair = item
        block_row = pair[0].astype(jnp.int32)
        block_col = pair[1].astype(jnp.int32)
        differ = block_row != block_col
        direct_tile = jnp.where(jnp.logical_or(lower, differ), tile, jnp.zeros_like(tile))
        mirror_tile = jnp.where(jnp.logical_or(strict, differ), tile, jnp.zeros_like(tile))
        row_start = (block_row * order).astype(jnp.int32)
        col_start = (block_col * order).astype(jnp.int32)
        from_col = lax.dynamic_slice_in_dim(field, col_start, order, 1)
        from_row = lax.dynamic_slice_in_dim(field, row_start, order, 1)
        into_row = lax.dot_general(from_col, direct_tile, (((1,), (1,)), ((), ())), precision=lax.Precision.HIGHEST, preferred_element_type=jnp.float32)
        into_col = jnp.dot(from_row, mirror_tile, precision=lax.Precision.HIGHEST, preferred_element_type=jnp.float32)
        total = lax.dynamic_update_slice_in_dim(total, lax.dynamic_slice_in_dim(total, row_start, order, 1) + into_row, row_start, 1)
        total = lax.dynamic_update_slice_in_dim(total, lax.dynamic_slice_in_dim(total, col_start, order, 1) + into_col, col_start, 1)
        return total, None

    start = jnp.zeros(field.shape, jnp.float32)
    total, _ = lax.scan(step, start, (tiles, tile_list))
    return total


def reference(right_side, ridge, tiles, tile_list):
    solution = jnp.zeros_like(right_side)
    residual = right_side
    direction = right_side
    norm_now = gram(residual, residual)
    for step in range(ITERS):
        image = apply_kernel(tiles, tile_list, direction) + ridge[None, :] * direction
        alpha = gauss_solve(gram(direction, image), norm_now)
        solution = solution + jnp.dot(alpha.T, direction, precision=lax.Precision.HIGHEST)
        residual = residual - jnp.dot(alpha.T, image, precision=lax.Precision.HIGHEST)
        if step + 1 < ITERS:
            norm_next = gram(residual, residual)
            beta = gauss_solve(norm_now, norm_next)
            direction = residual + jnp.dot(beta.T, direction, precision=lax.Precision.HIGHEST)
            norm_now = norm_next
    return solution, residual
```

```python
import functools

import jax
import jax.numpy as jnp
from jax import lax
from jax.experimental import pallas as pl
from jax.experimental.pallas import tpu as pltpu
from jax.sharding import PartitionSpec as P

ITERS = 2
MESH = pl.DeviceIdType.MESH
F32 = jnp.float32
BF16 = jnp.bfloat16
HIGH = lax.Precision.HIGHEST
NT_DIMS = (((1,), (1,)), ((), ()))


def split(x):
    hi = x.astype(BF16)
    lo = (x - hi.astype(F32)).astype(BF16)
    return jnp.concatenate([hi, lo], axis=0)


def fold(y):
    s = y.shape[0] // 2
    return y[:s] + y[s:]


def dot_nt(a, b):
    return lax.dot_general(a, b, NT_DIMS, preferred_element_type=F32)


def dot_nn(a, b):
    return jnp.dot(a, b, preferred_element_type=F32)


def gram_small(a, b):
    s = a.shape[0]
    g = dot_nt(split(a), split(b))
    g = g[:s] + g[s:]
    return g[:, :s] + g[:, s:]


def mixed(coeffs, rows):
    return jnp.dot(coeffs.T, rows, precision=HIGH, preferred_element_type=F32)


def gauss_solve(matrix, rhs):
    order = matrix.shape[0]
    aug = jnp.concatenate([matrix, rhs], axis=1)
    rows = lax.broadcasted_iota(jnp.int32, aug.shape, 0)
    for p in range(order):
        row_new = aug[p : p + 1, :] * (1.0 / aug[p : p + 1, p : p + 1])
        aug = jnp.where(rows == p, row_new, aug - aug[:, p : p + 1] * row_new)
    return aug[:, order:]


def kernel(
    grps, tiles_axis,
    list_ref, rhs_ref, ridge_ref, tiles_ref, sol_ref, res_ref,
    stage, high, low, field, image, parts, away, other0, other1, mine, came0, came1,
    small, small_sum, small_in, small_other,
    stage_sem, ag_send, ag_recv, fw_send, fw_recv, ex_send, ex_recv, rs_send, rs_recv,
    sm_send, sm_recv,
):
    half = tiles_axis // 2
    chips = grps * half
    grp = lax.axis_index("grp")
    tile = lax.axis_index("tile")
    core = lax.rem(tile, 2)
    chip = grp * half + tile // 2
    nt, order = tiles_ref.shape[0], tiles_ref.shape[1]
    s, width = rhs_ref.shape
    per = order // width

    def device(j, c):
        return (j // half, lax.rem(j, half) * 2 + c)

    partner = device(chip, 1 - core)

    def ahead(k):
        return lax.rem(chip + k, chips)

    def behind(k):
        return lax.rem(chip + chips - k, chips)

    def remote(src, dst, ssem, rsem, dev):
        return pltpu.make_async_remote_copy(
            src_ref=src, dst_ref=dst, send_sem=ssem, recv_sem=rsem, device_id=dev, device_id_type=MESH
        )

    def loads(t):
        return pltpu.make_async_copy(tiles_ref.at[t], stage.at[t], stage_sem.at[t])

    for t in range(nt):
        loads(t).start()

    barrier = pltpu.get_barrier_semaphore()
    pl.semaphore_signal(barrier, inc=1, device_id=partner, device_id_type=MESH)

    @pl.loop(1, chips)
    def _(k):
        pl.semaphore_signal(barrier, inc=1, device_id=device(ahead(k), core), device_id_type=MESH)

    pl.semaphore_wait(barrier, chips)

    def ag_copy(src, buf, it, k):
        return remote(src, buf.at[core, chip], ag_send.at[it, k], ag_recv.at[it, k], device(ahead(k), core))

    def fw_copy(src, buf, it, k):
        j = behind(k)
        return remote(src, buf.at[core, j], fw_send.at[it, k], fw_recv.at[it, k], partner)

    def gather_start(src, buf, it):
        @pl.loop(1, chips)
        def _(k):
            ag_copy(src, buf, it, k).start()

        fw_copy(src, buf, it, 0).start()

    def gather_forward(src, buf, it):
        @pl.loop(1, chips)
        def _(k):
            remote(
                src, buf.at[core, behind(k)], ag_send.at[it, k], ag_recv.at[it, k], device(ahead(k), core)
            ).wait_recv()
            fw_copy(buf.at[core, behind(k)], buf, it, k).start()

    def gather_finish(src, buf, it):
        @pl.loop(0, chips)
        def _(k):
            remote(
                src, buf.at[1 - core, behind(k)], fw_send.at[it, k], fw_recv.at[it, k], partner
            ).wait_recv()

        @pl.loop(1, chips)
        def _(k):
            ag_copy(src, buf, it, k).wait_send()
            fw_copy(buf.at[core, behind(k)], buf, it, k).wait_send()

        fw_copy(src, buf, it, 0).wait_send()

    def block(buf, b):
        pieces = []
        for i in range(per):
            p = b * per + i
            pieces.append(buf[lax.rem(p, 2), p // 2])
        return pieces[0] if per == 1 else jnp.concatenate(pieces, axis=1)

    def apply(buf, with_gram):
        total = jnp.zeros((s, s), F32)
        for t in range(nt):
            row_x = block(buf, list_ref[t, 0])
            row = split(row_x)
            col = split(block(buf, list_ref[t, 1]))
            into_row = fold(dot_nt(col, high[t]) + dot_nt(col, low[t]))
            parts[2 * t] = into_row
            parts[2 * t + 1] = fold(dot_nn(row, high[t]) + dot_nn(row, low[t]))
            if with_gram:
                g = gram_small(row_x, into_row)
                total = total + g + g.T
        return total

    def piece(p):
        b = p // per
        at = pl.ds(pl.multiple_of(lax.rem(p, per) * width, width), width)
        zero = jnp.zeros((s, width), F32)
        acc = zero
        for t in range(nt):
            acc = acc + jnp.where(list_ref[t, 0] == b, parts[2 * t, :, at], zero)
            acc = acc + jnp.where(list_ref[t, 1] == b, parts[2 * t + 1, :, at], zero)
        return acc

    def ex_copy(other, it, j):
        return remote(away.at[j], other.at[j], ex_send.at[it, j], ex_recv.at[it, j], partner)

    def rs_copy(came, it, k):
        return remote(
            mine.at[ahead(k)], came.at[k], rs_send.at[it, k], rs_recv.at[it, k], device(ahead(k), core)
        )

    def scatter_start(other, came, it):
        @pl.loop(1, chips + 1)
        def _(k):
            j = ahead(k)
            away[j] = piece(2 * j + 1 - core)
            ex_copy(other, it, j).start()

        @pl.loop(1, chips + 1)
        def _(k):
            j = ahead(k)
            mine[j] = piece(2 * j + core)

        @pl.loop(1, chips)
        def _(k):
            j = ahead(k)
            ex_copy(other, it, j).wait_recv()
            mine[j] = mine[j] + other[j]
            rs_copy(came, it, k).start()

        ex_copy(other, it, chip).wait_recv()

    def scatter_finish(other, came, it):
        def step(k, acc):
            rs_copy(came, it, k).wait_recv()
            return acc + came[k]

        total = lax.fori_loop(1, chips, step, mine[chip] + other[chip])

        @pl.loop(1, chips)
        def _(k):
            rs_copy(came, it, k).wait_send()

        @pl.loop(0, chips)
        def _(j):
            ex_copy(other, it, j).wait_send()

        return total

    def gram_all(first, second):
        def step(j, acc):
            for c in range(2):
                acc = acc + gram_small(first[c, j], second[c, j])
            return acc

        return lax.fori_loop(0, chips, step, jnp.zeros((s, s), F32), unroll=4)

    gather_start(rhs_ref, field, 0)
    field[core, chip] = rhs_ref[...]

    chunk = min(128, order)
    for t in range(nt):
        loads(t).wait()
        differ = list_ref[t, 0] != list_ref[t, 1]

        @pl.loop(0, order // chunk)
        def _(i):
            at = pl.ds(pl.multiple_of(i * chunk, chunk), chunk)
            x = stage[t, at, :]
            rows = lax.broadcasted_iota(jnp.int32, x.shape, 0) + i * chunk
            cols = lax.broadcasted_iota(jnp.int32, x.shape, 1)
            weight = jnp.where(rows > cols, 1.0, jnp.where(rows == cols, 0.5, 0.0))
            weight = jnp.where(differ, 1.0, weight)
            x = x * weight
            hi = x.astype(BF16)
            high[t, at, :] = hi
            low[t, at, :] = (x - hi.astype(F32)).astype(BF16)

    gather_forward(rhs_ref, field, 0)
    gather_finish(rhs_ref, field, 0)

    apply(field, False)
    scatter_start(other0, came0, 0)
    norm0 = gram_all(field, field)
    own_rhs = rhs_ref[...]
    own_ridge = ridge_ref[...]
    own_image = scatter_finish(other0, came0, 0) + own_ridge * own_rhs
    image[core, chip] = own_image
    gather_start(image.at[core, chip], image, 1)
    gather_forward(image.at[core, chip], image, 1)
    gather_finish(image.at[core, chip], image, 1)

    alpha = gauss_solve(gram_all(field, image), norm0)

    def residual_step(j, acc):
        for c in range(2):
            r = field[c, j] - mixed(alpha, image[c, j])
            image[c, j] = r
            acc = acc + gram_small(r, r)
        return acc

    norm1 = lax.fori_loop(0, chips, residual_step, jnp.zeros((s, s), F32), unroll=2)
    beta = gauss_solve(norm0, norm1)

    @pl.loop(0, chips, unroll=2)
    def _(j):
        for c in range(2):
            field[c, j] = image[c, j] + mixed(beta, field[c, j])

    partial = apply(field, True)
    own_dir = field[core, chip]
    partial = partial + gram_small(own_dir, own_dir * own_ridge)
    pad = jnp.concatenate([partial, jnp.zeros((s, 128 - s), F32)], axis=1)
    small[...] = pad
    sm_ex = remote(small, small_other, sm_send.at[0], sm_recv.at[0], partner)
    sm_ex.start()
    scatter_start(other1, came1, 1)
    sm_ex.wait_recv()
    small_sum[...] = pad + small_other[...]

    def sm_copy(k):
        return remote(small_sum, small_in.at[k], sm_send.at[k], sm_recv.at[k], device(ahead(k), core))

    @pl.loop(1, chips)
    def _(k):
        sm_copy(k).start()

    sol_ref[...] = mixed(alpha, own_rhs)

    def sm_step(k, acc):
        sm_copy(k).wait_recv()
        return acc + small_in[k]

    pq = lax.fori_loop(1, chips, sm_step, small_sum[...])[:, :s]
    alpha1 = gauss_solve(pq, norm1)
    sol_ref[...] = sol_ref[...] + mixed(alpha1, own_dir)
    last = scatter_finish(other1, came1, 1) + own_ridge * own_dir
    res_ref[...] = image[core, chip] - mixed(alpha1, last)

    @pl.loop(1, chips)
    def _(k):
        sm_copy(k).wait_send()

    sm_ex.wait_send()


def solution(mesh):
    grps, tiles_axis = mesh.shape["grp"], mesh.shape["tile"]
    chips = grps * tiles_axis // 2

    def local(right_side, ridge, tiles, tile_list):
        s, width = right_side.shape
        nt, order = tiles.shape[0], tiles.shape[1]
        vmem = pl.BlockSpec(memory_space=pltpu.VMEM)
        out = jax.ShapeDtypeStruct((s, width), F32)
        dma = pltpu.SemaphoreType.DMA
        return pl.pallas_call(
            functools.partial(kernel, grps, tiles_axis),
            out_shape=(out, out),
            in_specs=[
                pl.BlockSpec(memory_space=pltpu.SMEM),
                vmem,
                vmem,
                pl.BlockSpec(memory_space=pl.ANY),
            ],
            out_specs=(vmem, vmem),
            scratch_shapes=[
                pltpu.VMEM((nt, order, order), F32),
                pltpu.VMEM((nt, order, order), BF16),
                pltpu.VMEM((nt, order, order), BF16),
                pltpu.VMEM((2, chips, s, width), F32),
                pltpu.VMEM((2, chips, s, width), F32),
                pltpu.VMEM((2 * nt, s, order), F32),
                pltpu.VMEM((chips, s, width), F32),
                pltpu.VMEM((chips, s, width), F32),
                pltpu.VMEM((chips, s, width), F32),
                pltpu.VMEM((chips, s, width), F32),
                pltpu.VMEM((chips, s, width), F32),
                pltpu.VMEM((chips, s, width), F32),
                pltpu.VMEM((s, 128), F32),
                pltpu.VMEM((s, 128), F32),
                pltpu.VMEM((chips, s, 128), F32),
                pltpu.VMEM((s, 128), F32),
                dma((nt,)),
                dma((2, chips)),
                dma((2, chips)),
                dma((2, chips)),
                dma((2, chips)),
                dma((2, chips)),
                dma((2, chips)),
                dma((2, chips)),
                dma((2, chips)),
                dma((chips,)),
                dma((chips,)),
            ],
            compiler_params=pltpu.CompilerParams(
                collective_id=0, has_side_effects=True, vmem_limit_bytes=60 * 1024 * 1024
            ),
        )(tile_list, right_side, ridge[None, :], tiles)

    return jax.shard_map(
        local,
        mesh=mesh,
        in_specs=(
            P(None, ("grp", "tile")),
            P(("grp", "tile")),
            P(("grp", "tile"), None, None),
            P(("grp", "tile"), None),
        ),
        out_specs=(P(None, ("grp", "tile")), P(None, ("grp", "tile"))),
        check_vma=False,
    )
```

```python
import functools

import jax
import jax.numpy as jnp
from jax import lax
from jax.experimental import pallas as pl
from jax.experimental.pallas import tpu as pltpu
from jax.sharding import PartitionSpec as P

ITERS = 2
MESH = pl.DeviceIdType.MESH
F32 = jnp.float32
BF16 = jnp.bfloat16
HIGH = lax.Precision.HIGHEST
NT_DIMS = (((1,), (1,)), ((), ()))


def split(x):
    hi = x.astype(BF16)
    lo = (x - hi.astype(F32)).astype(BF16)
    return jnp.concatenate([hi, lo], axis=0)


def fold(y):
    s = y.shape[0] // 2
    return y[:s] + y[s:]


def dot_nt(a, b):
    return lax.dot_general(a, b, NT_DIMS, preferred_element_type=F32)


def dot_nn(a, b):
    return jnp.dot(a, b, preferred_element_type=F32)


def gram_small(a, b):
    s = a.shape[0]
    g = dot_nt(split(a), split(b))
    g = g[:s] + g[s:]
    return g[:, :s] + g[:, s:]


def mixed(coeffs, rows):
    return jnp.dot(coeffs.T, rows, precision=HIGH, preferred_element_type=F32)


def gauss_solve(matrix, rhs):
    order = matrix.shape[0]
    aug = jnp.concatenate([matrix, rhs], axis=1)
    rows = lax.broadcasted_iota(jnp.int32, aug.shape, 0)
    for p in range(order):
        row_new = aug[p : p + 1, :] * (1.0 / aug[p : p + 1, p : p + 1])
        aug = jnp.where(rows == p, row_new, aug - aug[:, p : p + 1] * row_new)
    return aug[:, order:]


def kernel(
    grps, tiles_axis,
    list_ref, rhs_ref, ridge_ref, tiles_ref, sol_ref, res_ref,
    stage, high, low, field, image, parts, away, other0, other1, mine, came0, came1,
    small, small_sum, small_in, small_other,
    stage_sem, agz_send, agz_recv, agq_send, agq_recv, fw_send, fw_recv, ex_send, ex_recv,
    rsz_send, rsz_recv, rsq_send, rsq_recv, sm_send, sm_recv, smq_send, smq_recv, smz_send, smz_recv,
):
    half = tiles_axis // 2
    chips = grps * half
    grp = lax.axis_index("grp")
    tile = lax.axis_index("tile")
    core = lax.rem(tile, 2)
    place = tile // 2
    chip = grp * half + place
    nt, order = tiles_ref.shape[0], tiles_ref.shape[1]
    s, width = rhs_ref.shape
    per = order // width

    def device(j, c):
        return (j // half, lax.rem(j, half) * 2 + c)

    partner = device(chip, 1 - core)

    def ahead(kz, kq):
        return lax.rem(grp + kz, grps) * half + lax.rem(place + kq, half)

    def behind(kz, kq):
        return lax.rem(grp + grps - kz, grps) * half + lax.rem(place + half - kq, half)

    def remote(src, dst, ssem, rsem, dev):
        return pltpu.make_async_remote_copy(
            src_ref=src, dst_ref=dst, send_sem=ssem, recv_sem=rsem, device_id=dev, device_id_type=MESH
        )

    def loads(t):
        return pltpu.make_async_copy(tiles_ref.at[t], stage.at[t], stage_sem.at[t])

    for t in range(nt):
        loads(t).start()

    barrier = pltpu.get_barrier_semaphore()
    pl.semaphore_signal(barrier, inc=1, device_id=partner, device_id_type=MESH)

    for kz in range(1, grps):
        pl.semaphore_signal(barrier, inc=1, device_id=device(ahead(kz, 0), core), device_id_type=MESH)
    for kq in range(1, half):
        pl.semaphore_signal(barrier, inc=1, device_id=device(ahead(0, kq), core), device_id_type=MESH)
    pl.semaphore_wait(barrier, grps + half - 1)

    def ag_z(src, buf, it, kz):
        return remote(src, buf.at[core, chip], agz_send.at[it, kz], agz_recv.at[it, kz], device(ahead(kz, 0), core))

    def ag_q(src, buf, it, kz, kq):
        return remote(
            src, buf.at[core, behind(kz, 0)], agq_send.at[it, kz, kq], agq_recv.at[it, kz, kq], device(ahead(0, kq), core)
        )

    def fw_copy(src, buf, it, kz, kq):
        return remote(src, buf.at[core, behind(kz, kq)], fw_send.at[it, kz, kq], fw_recv.at[it, kz, kq], partner)

    def spread(src, buf, it, kz):
        for kq in range(1, half):
            ag_q(src, buf, it, kz, kq).start()
        fw_copy(src, buf, it, kz, 0).start()

    def gather_start(src, buf, it):
        for kz in range(1, grps):
            ag_z(src, buf, it, kz).start()
        spread(src, buf, it, 0)

    def gather_spread(buf, it, kz):
        mine_now = buf.at[core, behind(kz, 0)]
        remote(
            mine_now, mine_now, agz_send.at[it, kz], agz_recv.at[it, kz], device(ahead(kz, 0), core)
        ).wait_recv()
        spread(mine_now, buf, it, kz)

    def gather_forward(buf, it):
        for kz in range(grps):
            for kq in range(1, half):
                mine_now = buf.at[core, behind(kz, kq)]
                remote(
                    mine_now, mine_now, agq_send.at[it, kz, kq], agq_recv.at[it, kz, kq], device(ahead(0, kq), core)
                ).wait_recv()
                fw_copy(mine_now, buf, it, kz, kq).start()

    def gather_finish(src, buf, it):
        for kz in range(grps):
            for kq in range(half):
                other_now = buf.at[1 - core, behind(kz, kq)]
                remote(other_now, other_now, fw_send.at[it, kz, kq], fw_recv.at[it, kz, kq], partner).wait_recv()
        for kz in range(grps):
            held = src if kz == 0 else buf.at[core, behind(kz, 0)]
            if kz > 0:
                ag_z(src, buf, it, kz).wait_send()
            for kq in range(half):
                if kq > 0:
                    ag_q(held, buf, it, kz, kq).wait_send()
                fw_copy(held if kq == 0 else buf.at[core, behind(kz, kq)], buf, it, kz, kq).wait_send()

    def block(buf, b):
        pieces = []
        for i in range(per):
            p = b * per + i
            pieces.append(buf[lax.rem(p, 2), p // 2])
        return pieces[0] if per == 1 else jnp.concatenate(pieces, axis=1)

    def apply(buf, with_gram):
        total = jnp.zeros((s, s), F32)
        for t in range(nt):
            row_x = block(buf, list_ref[t, 0])
            row = split(row_x)
            col = split(block(buf, list_ref[t, 1]))
            into_row = fold(dot_nt(col, high[t]) + dot_nt(col, low[t]))
            parts[2 * t] = into_row
            parts[2 * t + 1] = fold(dot_nn(row, high[t]) + dot_nn(row, low[t]))
            if with_gram:
                g = gram_small(row_x, into_row)
                total = total + g + g.T
        return total

    def piece(p):
        b = p // per
        at = pl.ds(pl.multiple_of(lax.rem(p, per) * width, width), width)
        zero = jnp.zeros((s, width), F32)
        acc = zero
        for t in range(nt):
            acc = acc + jnp.where(list_ref[t, 0] == b, parts[2 * t, :, at], zero)
            acc = acc + jnp.where(list_ref[t, 1] == b, parts[2 * t + 1, :, at], zero)
        return acc

    def ex_copy(other, it, j):
        return remote(away.at[j], other.at[j], ex_send.at[it, j], ex_recv.at[it, j], partner)

    def rsq_copy(came, it, kz, kq):
        return remote(
            mine.at[ahead(kz, kq)], came.at[kz, kq], rsq_send.at[it, kz, kq], rsq_recv.at[it, kz, kq],
            device(ahead(0, kq), core),
        )

    def rsz_copy(came, it, kz):
        return remote(
            mine.at[ahead(kz, 0)], came.at[kz, 0], rsz_send.at[it, kz], rsz_recv.at[it, kz],
            device(ahead(kz, 0), core),
        )

    zs = list(range(1, grps)) + [0]
    qs = list(range(1, half)) + [0]

    def scatter_start(other, came, it):
        def order_of(i):
            return ahead(lax.rem(i // half + 1, grps), lax.rem(lax.rem(i, half) + 1, half))

        @pl.loop(0, chips)
        def _(i):
            j = order_of(i)
            away[j] = piece(2 * j + 1 - core)
            ex_copy(other, it, j).start()

        @pl.loop(0, chips)
        def _(i):
            j = order_of(i)
            mine[j] = piece(2 * j + core)

        for kz in zs:
            for kq in qs:
                j = ahead(kz, kq)
                ex_copy(other, it, j).wait_recv()
                mine[j] = mine[j] + other[j]
                if kq > 0:
                    rsq_copy(came, it, kz, kq).start()

    def scatter_columns(came, it):
        for kz in zs:
            j = ahead(kz, 0)
            acc = mine[j]
            for kq in range(1, half):
                rsq_copy(came, it, kz, kq).wait_recv()
                acc = acc + came[kz, kq]
            mine[j] = acc
            if kz > 0:
                rsz_copy(came, it, kz).start()

    def scatter_finish(came, it):
        total = mine[chip]
        for kz in range(1, grps):
            rsz_copy(came, it, kz).wait_recv()
            total = total + came[kz, 0]
        for kz in range(grps):
            if kz > 0:
                rsz_copy(came, it, kz).wait_send()
            for kq in range(half):
                if kq > 0:
                    rsq_copy(came, it, kz, kq).wait_send()
                ex_copy(other0, it, ahead(kz, kq)).wait_send()
        return total

    def gram_all(first, second):
        def step(j, acc):
            for c in range(2):
                acc = acc + gram_small(first[c, j], second[c, j])
            return acc

        return lax.fori_loop(0, chips, step, jnp.zeros((s, s), F32), unroll=4)

    gather_start(rhs_ref, field, 0)
    field[core, chip] = rhs_ref[...]

    chunk = min(128, order)

    def prepare(t):
        loads(t).wait()
        differ = list_ref[t, 0] != list_ref[t, 1]

        @pl.loop(0, order // chunk)
        def _(i):
            at = pl.ds(pl.multiple_of(i * chunk, chunk), chunk)
            x = stage[t, at, :]
            rows = lax.broadcasted_iota(jnp.int32, x.shape, 0) + i * chunk
            cols = lax.broadcasted_iota(jnp.int32, x.shape, 1)
            weight = jnp.where(rows > cols, 1.0, jnp.where(rows == cols, 0.5, 0.0))
            weight = jnp.where(differ, 1.0, weight)
            x = x * weight
            hi = x.astype(BF16)
            high[t, at, :] = hi
            low[t, at, :] = (x - hi.astype(F32)).astype(BF16)

    for i in range(max(nt, grps - 1)):
        if i < nt:
            prepare(i)
        if i + 1 < grps:
            gather_spread(field, 0, i + 1)
    gather_forward(field, 0)
    gather_finish(rhs_ref, field, 0)

    apply(field, False)
    scatter_start(other0, came0, 0)
    scatter_columns(came0, 0)
    norm0 = gram_all(field, field)
    own_rhs = rhs_ref[...]
    own_ridge = ridge_ref[...]
    own_image = scatter_finish(came0, 0) + own_ridge * own_rhs
    image[core, chip] = own_image
    gather_start(image.at[core, chip], image, 1)
    for kz in range(1, grps):
        gather_spread(image, 1, kz)
    gather_forward(image, 1)
    gather_finish(image.at[core, chip], image, 1)

    alpha = gauss_solve(gram_all(field, image), norm0)

    def residual_step(j, acc):
        for c in range(2):
            r = field[c, j] - mixed(alpha, image[c, j])
            image[c, j] = r
            acc = acc + gram_small(r, r)
        return acc

    norm1 = lax.fori_loop(0, chips, residual_step, jnp.zeros((s, s), F32), unroll=2)
    beta = gauss_solve(norm0, norm1)

    @pl.loop(0, chips, unroll=2)
    def _(j):
        for c in range(2):
            field[c, j] = image[c, j] + mixed(beta, field[c, j])

    partial = apply(field, True)
    own_dir = field[core, chip]
    partial = partial + gram_small(own_dir, own_dir * own_ridge)
    pad = jnp.concatenate([partial, jnp.zeros((s, 128 - s), F32)], axis=1)
    small[...] = pad
    sm_ex = remote(small, small_other, sm_send.at[0], sm_recv.at[0], partner)
    sm_ex.start()
    scatter_start(other1, came1, 1)
    sm_ex.wait_recv()
    small_sum[0] = pad + small_other[...]

    def smq_copy(kq):
        return remote(
            small_sum.at[0], small_in.at[0, kq], smq_send.at[kq], smq_recv.at[kq], device(ahead(0, kq), core)
        )

    def smz_copy(kz):
        return remote(
            small_sum.at[1], small_in.at[1, kz], smz_send.at[kz], smz_recv.at[kz], device(ahead(kz, 0), core)
        )

    for kq in range(1, half):
        smq_copy(kq).start()
    acc = small_sum[0]
    for kq in range(1, half):
        smq_copy(kq).wait_recv()
        acc = acc + small_in[0, kq]
    small_sum[1] = acc
    for kz in range(1, grps):
        smz_copy(kz).start()
    scatter_columns(came1, 1)
    sol_ref[...] = mixed(alpha, own_rhs)
    for kz in range(1, grps):
        smz_copy(kz).wait_recv()
        acc = acc + small_in[1, kz]
    pq = acc[:, :s]
    alpha1 = gauss_solve(pq, norm1)
    sol_ref[...] = sol_ref[...] + mixed(alpha1, own_dir)
    last = scatter_finish(came1, 1) + own_ridge * own_dir
    res_ref[...] = image[core, chip] - mixed(alpha1, last)

    for kq in range(1, half):
        smq_copy(kq).wait_send()
    for kz in range(1, grps):
        smz_copy(kz).wait_send()
    sm_ex.wait_send()


def solution(mesh):
    grps, tiles_axis = mesh.shape["grp"], mesh.shape["tile"]
    half = tiles_axis // 2
    chips = grps * half

    def local(right_side, ridge, tiles, tile_list):
        s, width = right_side.shape
        nt, order = tiles.shape[0], tiles.shape[1]
        vmem = pl.BlockSpec(memory_space=pltpu.VMEM)
        out = jax.ShapeDtypeStruct((s, width), F32)
        dma = pltpu.SemaphoreType.DMA
        return pl.pallas_call(
            functools.partial(kernel, grps, tiles_axis),
            out_shape=(out, out),
            in_specs=[
                pl.BlockSpec(memory_space=pltpu.SMEM),
                vmem,
                vmem,
                pl.BlockSpec(memory_space=pl.ANY),
            ],
            out_specs=(vmem, vmem),
            scratch_shapes=[
                pltpu.VMEM((nt, order, order), F32),
                pltpu.VMEM((nt, order, order), BF16),
                pltpu.VMEM((nt, order, order), BF16),
                pltpu.VMEM((2, chips, s, width), F32),
                pltpu.VMEM((2, chips, s, width), F32),
                pltpu.VMEM((2 * nt, s, order), F32),
                pltpu.VMEM((chips, s, width), F32),
                pltpu.VMEM((chips, s, width), F32),
                pltpu.VMEM((chips, s, width), F32),
                pltpu.VMEM((chips, s, width), F32),
                pltpu.VMEM((grps, half, s, width), F32),
                pltpu.VMEM((grps, half, s, width), F32),
                pltpu.VMEM((s, 128), F32),
                pltpu.VMEM((2, s, 128), F32),
                pltpu.VMEM((2, max(half, grps), s, 128), F32),
                pltpu.VMEM((s, 128), F32),
                dma((nt,)),
                dma((2, grps)),
                dma((2, grps)),
                dma((2, grps, half)),
                dma((2, grps, half)),
                dma((2, grps, half)),
                dma((2, grps, half)),
                dma((2, chips)),
                dma((2, chips)),
                dma((2, grps)),
                dma((2, grps)),
                dma((2, grps, half)),
                dma((2, grps, half)),
                dma((1,)),
                dma((1,)),
                dma((half,)),
                dma((half,)),
                dma((grps,)),
                dma((grps,)),
            ],
            compiler_params=pltpu.CompilerParams(
                collective_id=0, has_side_effects=True, vmem_limit_bytes=60 * 1024 * 1024
            ),
        )(tile_list, right_side, ridge[None, :], tiles)

    return jax.shard_map(
        local,
        mesh=mesh,
        in_specs=(
            P(None, ("grp", "tile")),
            P(("grp", "tile")),
            P(("grp", "tile"), None, None),
            P(("grp", "tile"), None),
        ),
        out_specs=(P(None, ("grp", "tile")), P(None, ("grp", "tile"))),
        check_vma=False,
    )
```

```python
import functools

import jax
import jax.numpy as jnp
from jax import lax
from jax.experimental import pallas as pl
from jax.experimental.pallas import tpu as pltpu
from jax.sharding import PartitionSpec as P

ITERS = 2
MESH = pl.DeviceIdType.MESH
F32 = jnp.float32
BF16 = jnp.bfloat16
HIGH = lax.Precision.HIGHEST
NT_DIMS = (((1,), (1,)), ((), ()))


def split(x):
    hi = x.astype(BF16)
    lo = (x - hi.astype(F32)).astype(BF16)
    return jnp.concatenate([hi, lo], axis=0)


def fold(y):
    s = y.shape[0] // 2
    return y[:s] + y[s:]


def dot_nt(a, b):
    return lax.dot_general(a, b, NT_DIMS, preferred_element_type=F32)


def dot_nn(a, b):
    return jnp.dot(a, b, preferred_element_type=F32)


def gram_small(a, b):
    s = a.shape[0]
    g = dot_nt(split(a), split(b))
    g = g[:s] + g[s:]
    return g[:, :s] + g[:, s:]


def mixed(coeffs_t, rows):
    return jnp.dot(coeffs_t, rows, precision=HIGH, preferred_element_type=F32)


def gauss_solve(matrix, rhs):
    order = matrix.shape[0]
    aug = jnp.concatenate([matrix, rhs], axis=1)
    rows = lax.broadcasted_iota(jnp.int32, aug.shape, 0)
    for p in range(order):
        row_new = aug[p : p + 1, :] * (1.0 / aug[p : p + 1, p : p + 1])
        aug = jnp.where(rows == p, row_new, aug - aug[:, p : p + 1] * row_new)
    return aug[:, order:]


def kernel(
    grps, tiles_axis,
    list_ref, rhs_ref, ridge_ref, tiles_ref, sol_ref, res_ref,
    stage, high, low, field, image, parts0, parts1, away, other0, other1, mine, came0, came1,
    small, small_sum, small_in, small_other,
    stage_sem, agz_send, agz_recv, agq_send, agq_recv, fw_send, fw_recv, ex_send, ex_recv,
    rsz_send, rsz_recv, rsq_send, rsq_recv, sm_send, sm_recv, smq_send, smq_recv, smz_send, smz_recv,
):
    half = tiles_axis // 2
    chips = grps * half
    grp = lax.axis_index("grp")
    tile = lax.axis_index("tile")
    core = lax.rem(tile, 2)
    place = tile // 2
    chip = grp * half + place
    nt, order = tiles_ref.shape[0], tiles_ref.shape[1]
    s, width = rhs_ref.shape
    per = order // width

    def device(j, c):
        return (j // half, lax.rem(j, half) * 2 + c)

    partner = device(chip, 1 - core)

    def ahead(kz, kq):
        return lax.rem(grp + kz, grps) * half + lax.rem(place + kq, half)

    def behind(kz, kq):
        return lax.rem(grp + grps - kz, grps) * half + lax.rem(place + half - kq, half)

    def remote(src, dst, ssem, rsem, dev):
        return pltpu.make_async_remote_copy(
            src_ref=src, dst_ref=dst, send_sem=ssem, recv_sem=rsem, device_id=dev, device_id_type=MESH
        )

    def loads(t):
        return pltpu.make_async_copy(tiles_ref.at[t], stage.at[t], stage_sem.at[t])

    for t in range(nt):
        loads(t).start()

    barrier = pltpu.get_barrier_semaphore()
    pl.semaphore_signal(barrier, inc=1, device_id=partner, device_id_type=MESH)

    for kz in range(1, grps):
        pl.semaphore_signal(barrier, inc=1, device_id=device(ahead(kz, 0), core), device_id_type=MESH)
    for kq in range(1, half):
        pl.semaphore_signal(barrier, inc=1, device_id=device(ahead(0, kq), core), device_id_type=MESH)
    pl.semaphore_wait(barrier, grps + half - 1)

    def ag_z(src, buf, it, kz):
        return remote(src, buf.at[core, chip], agz_send.at[it, kz], agz_recv.at[it, kz], device(ahead(kz, 0), core))

    def ag_q(src, buf, it, kz, kq):
        return remote(
            src, buf.at[core, behind(kz, 0)], agq_send.at[it, kz, kq], agq_recv.at[it, kz, kq], device(ahead(0, kq), core)
        )

    def fw_copy(src, buf, it, kz, kq):
        return remote(src, buf.at[core, behind(kz, kq)], fw_send.at[it, kz, kq], fw_recv.at[it, kz, kq], partner)

    def spread(src, buf, it, kz):
        for kq in range(1, half):
            ag_q(src, buf, it, kz, kq).start()
        fw_copy(src, buf, it, kz, 0).start()

    def gather_start(src, buf, it):
        for kz in range(1, grps):
            ag_z(src, buf, it, kz).start()
        spread(src, buf, it, 0)

    def gather_spread(buf, it, kz):
        mine_now = buf.at[core, behind(kz, 0)]
        remote(
            mine_now, mine_now, agz_send.at[it, kz], agz_recv.at[it, kz], device(ahead(kz, 0), core)
        ).wait_recv()
        spread(mine_now, buf, it, kz)

    def gather_forward(buf, it, meet, acc):
        for kz in range(grps):
            for kq in range(1, half):
                j = behind(kz, kq)
                mine_now = buf.at[core, j]
                remote(
                    mine_now, mine_now, agq_send.at[it, kz, kq], agq_recv.at[it, kz, kq], device(ahead(0, kq), core)
                ).wait_recv()
                fw_copy(mine_now, buf, it, kz, kq).start()
                acc = meet(acc, core, j)
        return acc

    def gather_finish(src, buf, it, meet, acc):
        for kz in range(grps):
            for kq in range(half):
                j = behind(kz, kq)
                other_now = buf.at[1 - core, j]
                remote(other_now, other_now, fw_send.at[it, kz, kq], fw_recv.at[it, kz, kq], partner).wait_recv()
                acc = meet(acc, 1 - core, j)
        for kz in range(grps):
            held = src if kz == 0 else buf.at[core, behind(kz, 0)]
            if kz > 0:
                ag_z(src, buf, it, kz).wait_send()
            for kq in range(half):
                if kq > 0:
                    ag_q(held, buf, it, kz, kq).wait_send()
                fw_copy(held if kq == 0 else buf.at[core, behind(kz, kq)], buf, it, kz, kq).wait_send()
        return acc

    def block(buf, b):
        pieces = []
        for i in range(per):
            p = b * per + i
            pieces.append(buf[lax.rem(p, 2), p // 2])
        return pieces[0] if per == 1 else jnp.concatenate(pieces, axis=1)

    def apply(buf, parts):
        for t in range(nt):
            row = split(block(buf, list_ref[t, 0]))
            col = split(block(buf, list_ref[t, 1]))
            parts[2 * t] = fold(dot_nt(col, high[t]) + dot_nt(col, low[t]))
            parts[2 * t + 1] = fold(dot_nn(row, high[t]) + dot_nn(row, low[t]))

    def piece(p, parts):
        b = p // per
        at = pl.ds(pl.multiple_of(lax.rem(p, per) * width, width), width)
        zero = jnp.zeros((s, width), F32)
        acc = zero
        for t in range(nt):
            acc = acc + jnp.where(list_ref[t, 0] == b, parts[2 * t, :, at], zero)
            acc = acc + jnp.where(list_ref[t, 1] == b, parts[2 * t + 1, :, at], zero)
        return acc

    def ex_copy(other, it, j):
        return remote(away.at[j], other.at[j], ex_send.at[it, j], ex_recv.at[it, j], partner)

    def rsq_copy(came, it, kz, kq):
        return remote(
            mine.at[ahead(kz, kq)], came.at[kz, kq], rsq_send.at[it, kz, kq], rsq_recv.at[it, kz, kq],
            device(ahead(0, kq), core),
        )

    def rsz_copy(came, it, kz):
        return remote(
            mine.at[ahead(kz, 0)], came.at[kz, 0], rsz_send.at[it, kz], rsz_recv.at[it, kz],
            device(ahead(kz, 0), core),
        )

    zs = list(range(1, grps)) + [0]
    qs = list(range(1, half)) + [0]

    def scatter_start(other, came, it, parts):
        def order_of(i):
            return ahead(lax.rem(i // half + 1, grps), lax.rem(lax.rem(i, half) + 1, half))

        @pl.loop(0, chips)
        def _(i):
            j = order_of(i)
            away[j] = piece(2 * j + 1 - core, parts)
            ex_copy(other, it, j).start()

        @pl.loop(0, chips)
        def _(i):
            j = order_of(i)
            mine[j] = piece(2 * j + core, parts)

        for kz in zs:
            for kq in qs:
                j = ahead(kz, kq)
                ex_copy(other, it, j).wait_recv()
                mine[j] = mine[j] + other[j]
                if kq > 0:
                    rsq_copy(came, it, kz, kq).start()

    def scatter_columns(came, it):
        for kz in zs:
            j = ahead(kz, 0)
            acc = mine[j]
            for kq in range(1, half):
                rsq_copy(came, it, kz, kq).wait_recv()
                acc = acc + came[kz, kq]
            mine[j] = acc
            if kz > 0:
                rsz_copy(came, it, kz).start()

    def scatter_finish(came, it):
        total = mine[chip]
        for kz in range(1, grps):
            rsz_copy(came, it, kz).wait_recv()
            total = total + came[kz, 0]
        for kz in range(grps):
            if kz > 0:
                rsz_copy(came, it, kz).wait_send()
            for kq in range(half):
                if kq > 0:
                    rsq_copy(came, it, kz, kq).wait_send()
                ex_copy(other0, it, ahead(kz, kq)).wait_send()
        return total

    def gram_all(first, second):
        def step(j, acc):
            for c in range(2):
                acc = acc + gram_small(first[c, j], second[c, j])
            return acc

        return lax.fori_loop(0, chips, step, jnp.zeros((s, s), F32), unroll=4)

    gather_start(rhs_ref, field, 0)
    field[core, chip] = rhs_ref[...]

    chunk = min(128, order)

    def prepare(t):
        loads(t).wait()
        differ = list_ref[t, 0] != list_ref[t, 1]

        @pl.loop(0, order // chunk)
        def _(i):
            at = pl.ds(pl.multiple_of(i * chunk, chunk), chunk)
            x = stage[t, at, :]
            rows = lax.broadcasted_iota(jnp.int32, x.shape, 0) + i * chunk
            cols = lax.broadcasted_iota(jnp.int32, x.shape, 1)
            weight = jnp.where(rows > cols, 1.0, jnp.where(rows == cols, 0.5, 0.0))
            weight = jnp.where(differ, 1.0, weight)
            x = x * weight
            hi = x.astype(BF16)
            high[t, at, :] = hi
            low[t, at, :] = (x - hi.astype(F32)).astype(BF16)

    for i in range(max(nt, grps - 1)):
        if i < nt:
            prepare(i)
        if i + 1 < grps:
            gather_spread(field, 0, i + 1)
    def nothing(acc, c, j):
        return acc

    gather_forward(field, 0, nothing, None)
    gather_finish(rhs_ref, field, 0, nothing, None)

    apply(field, parts0)
    scatter_start(other0, came0, 0, parts0)
    norm0 = gram_all(field, field)
    scatter_columns(came0, 0)
    own_rhs = rhs_ref[...]
    own_ridge = ridge_ref[...]
    own_image = scatter_finish(came0, 0) + own_ridge * own_rhs
    image[core, chip] = own_image
    gather_start(image.at[core, chip], image, 1)

    def meet(acc, c, j):
        return acc + gram_small(field[c, j], image[c, j])

    pq = gram_small(own_rhs, own_image)
    for kz in range(1, grps):
        gather_spread(image, 1, kz)
        pq = meet(pq, core, behind(kz, 0))
    pq = gather_forward(image, 1, meet, pq)
    pq = gather_finish(image.at[core, chip], image, 1, meet, pq)

    apply(image, parts1)
    scatter_start(other1, came1, 1, parts1)
    alpha = gauss_solve(pq, norm0)
    alpha_t = alpha.T

    def residual_step(j, acc):
        for c in range(2):
            r = field[c, j] - mixed(alpha_t, image[c, j])
            acc = acc + gram_small(r, r)
        return acc

    norm1 = lax.fori_loop(0, chips, residual_step, jnp.zeros((s, s), F32), unroll=2)
    beta = gauss_solve(norm0, norm1)
    beta_t = beta.T

    def onward(first, second):
        return (first - mixed(alpha_t, second)) + mixed(beta_t, first)

    own_res = own_rhs - mixed(alpha_t, own_image)
    own_dir = own_res + mixed(beta_t, own_rhs)
    partial = gram_small(own_dir, own_dir * own_ridge)
    for t in range(nt):
        b = list_ref[t, 0]
        g = gram_small(onward(block(field, b), block(image, b)), onward(parts0[2 * t], parts1[2 * t]))
        partial = partial + g + g.T
    pad = jnp.concatenate([partial, jnp.zeros((s, 128 - s), F32)], axis=1)
    small[...] = pad
    sm_ex = remote(small, small_other, sm_send.at[0], sm_recv.at[0], partner)
    sm_ex.start()
    scatter_columns(came1, 1)
    sm_ex.wait_recv()
    small_sum[0] = pad + small_other[...]

    def smq_copy(kq):
        return remote(
            small_sum.at[0], small_in.at[0, kq], smq_send.at[kq], smq_recv.at[kq], device(ahead(0, kq), core)
        )

    def smz_copy(kz):
        return remote(
            small_sum.at[1], small_in.at[1, kz], smz_send.at[kz], smz_recv.at[kz], device(ahead(kz, 0), core)
        )

    for kq in range(1, half):
        smq_copy(kq).start()
    acc = small_sum[0]
    for kq in range(1, half):
        smq_copy(kq).wait_recv()
        acc = acc + small_in[0, kq]
    small_sum[1] = acc
    for kz in range(1, grps):
        smz_copy(kz).start()
    sol_ref[...] = mixed(alpha_t, own_rhs)
    for kz in range(1, grps):
        smz_copy(kz).wait_recv()
        acc = acc + small_in[1, kz]
    alpha1_t = gauss_solve(acc[:, :s], norm1).T
    sol_ref[...] = sol_ref[...] + mixed(alpha1_t, own_dir)
    spread_image = scatter_finish(came1, 1) + own_ridge * own_image
    res_ref[...] = own_res - mixed(alpha1_t, onward(own_image, spread_image))

    for kq in range(1, half):
        smq_copy(kq).wait_send()
    for kz in range(1, grps):
        smz_copy(kz).wait_send()
    sm_ex.wait_send()


def solution(mesh):
    grps, tiles_axis = mesh.shape["grp"], mesh.shape["tile"]
    half = tiles_axis // 2
    chips = grps * half

    def local(right_side, ridge, tiles, tile_list):
        s, width = right_side.shape
        nt, order = tiles.shape[0], tiles.shape[1]
        vmem = pl.BlockSpec(memory_space=pltpu.VMEM)
        out = jax.ShapeDtypeStruct((s, width), F32)
        dma = pltpu.SemaphoreType.DMA
        return pl.pallas_call(
            functools.partial(kernel, grps, tiles_axis),
            out_shape=(out, out),
            in_specs=[
                pl.BlockSpec(memory_space=pltpu.SMEM),
                vmem,
                vmem,
                pl.BlockSpec(memory_space=pl.ANY),
            ],
            out_specs=(vmem, vmem),
            scratch_shapes=[
                pltpu.VMEM((nt, order, order), F32),
                pltpu.VMEM((nt, order, order), BF16),
                pltpu.VMEM((nt, order, order), BF16),
                pltpu.VMEM((2, chips, s, width), F32),
                pltpu.VMEM((2, chips, s, width), F32),
                pltpu.VMEM((2 * nt, s, order), F32),
                pltpu.VMEM((2 * nt, s, order), F32),
                pltpu.VMEM((chips, s, width), F32),
                pltpu.VMEM((chips, s, width), F32),
                pltpu.VMEM((chips, s, width), F32),
                pltpu.VMEM((chips, s, width), F32),
                pltpu.VMEM((grps, half, s, width), F32),
                pltpu.VMEM((grps, half, s, width), F32),
                pltpu.VMEM((s, 128), F32),
                pltpu.VMEM((2, s, 128), F32),
                pltpu.VMEM((2, max(half, grps), s, 128), F32),
                pltpu.VMEM((s, 128), F32),
                dma((nt,)),
                dma((2, grps)),
                dma((2, grps)),
                dma((2, grps, half)),
                dma((2, grps, half)),
                dma((2, grps, half)),
                dma((2, grps, half)),
                dma((2, chips)),
                dma((2, chips)),
                dma((2, grps)),
                dma((2, grps)),
                dma((2, grps, half)),
                dma((2, grps, half)),
                dma((1,)),
                dma((1,)),
                dma((half,)),
                dma((half,)),
                dma((grps,)),
                dma((grps,)),
            ],
            compiler_params=pltpu.CompilerParams(
                collective_id=0, has_side_effects=True, vmem_limit_bytes=60 * 1024 * 1024
            ),
        )(tile_list, right_side, ridge[None, :], tiles)

    return jax.shard_map(
        local,
        mesh=mesh,
        in_specs=(
            P(None, ("grp", "tile")),
            P(("grp", "tile")),
            P(("grp", "tile"), None, None),
            P(("grp", "tile"), None),
        ),
        out_specs=(P(None, ("grp", "tile")), P(None, ("grp", "tile"))),
        check_vma=False,
    )
```

```python
import functools

import jax
import jax.numpy as jnp
from jax import lax
from jax.experimental import pallas as pl
from jax.experimental.pallas import tpu as pltpu
from jax.sharding import PartitionSpec as P

ITERS = 2
MESH = pl.DeviceIdType.MESH
F32 = jnp.float32
BF16 = jnp.bfloat16
HIGH = lax.Precision.HIGHEST
NT_DIMS = (((1,), (1,)), ((), ()))


def split(x):
    hi = x.astype(BF16)
    lo = (x - hi.astype(F32)).astype(BF16)
    return jnp.concatenate([hi, lo], axis=0)


def fold(y):
    s = y.shape[0] // 2
    return y[:s] + y[s:]


def dot_nt(a, b):
    return lax.dot_general(a, b, NT_DIMS, preferred_element_type=F32)


def dot_nn(a, b):
    return jnp.dot(a, b, preferred_element_type=F32)


def gram_small(a, b):
    s = a.shape[0]
    g = dot_nt(split(a), split(b))
    g = g[:s] + g[s:]
    return g[:, :s] + g[:, s:]


def terms(x):
    h = x.astype(BF16).astype(F32)
    m = (x - h).astype(BF16).astype(F32)
    return h, m, x - h - m


def mixer(coeffs_t):
    h, m, l = terms(coeffs_t)
    return jnp.concatenate([h, h, m, m, h, l], axis=1).astype(BF16)


def mixed(coeffs, rows):
    h, m, l = (x.astype(BF16) for x in terms(rows))
    return dot_nn(coeffs, jnp.concatenate([h, m, h, m, l, h], axis=0))


def gauss_solve(matrix, rhs):
    order = matrix.shape[0]
    aug = jnp.concatenate([matrix, rhs], axis=1)
    rows = lax.broadcasted_iota(jnp.int32, aug.shape, 0)
    for p in range(order):
        row_new = aug[p : p + 1, :] * (1.0 / aug[p : p + 1, p : p + 1])
        aug = jnp.where(rows == p, row_new, aug - aug[:, p : p + 1] * row_new)
    return aug[:, order:]


def kernel(
    grps, tiles_axis,
    list_ref, rhs_ref, ridge_ref, tiles_ref, sol_ref, res_ref,
    stage, high, low, field, image, parts0, parts1, away, other0, other1, mine, came0, came1,
    small, small_sum, small_in, small_other,
    stage_sem, agz_send, agz_recv, agq_send, agq_recv, fw_send, fw_recv, ex_send, ex_recv,
    rsz_send, rsz_recv, rsq_send, rsq_recv, sm_send, sm_recv, smq_send, smq_recv, smz_send, smz_recv,
):
    half = tiles_axis // 2
    chips = grps * half
    grp = lax.axis_index("grp")
    tile = lax.axis_index("tile")
    core = lax.rem(tile, 2)
    place = tile // 2
    chip = grp * half + place
    nt, order = tiles_ref.shape[0], tiles_ref.shape[1]
    s, width = rhs_ref.shape
    per = order // width

    def device(j, c):
        return (j // half, lax.rem(j, half) * 2 + c)

    partner = device(chip, 1 - core)

    def ahead(kz, kq):
        return lax.rem(grp + kz, grps) * half + lax.rem(place + kq, half)

    def behind(kz, kq):
        return lax.rem(grp + grps - kz, grps) * half + lax.rem(place + half - kq, half)

    def remote(src, dst, ssem, rsem, dev):
        return pltpu.make_async_remote_copy(
            src_ref=src, dst_ref=dst, send_sem=ssem, recv_sem=rsem, device_id=dev, device_id_type=MESH
        )

    def loads(t):
        return pltpu.make_async_copy(tiles_ref.at[t], stage.at[t], stage_sem.at[t])

    for t in range(nt):
        loads(t).start()

    barrier = pltpu.get_barrier_semaphore()
    pl.semaphore_signal(barrier, inc=1, device_id=partner, device_id_type=MESH)

    for kz in range(1, grps):
        pl.semaphore_signal(barrier, inc=1, device_id=device(ahead(kz, 0), core), device_id_type=MESH)
    for kq in range(1, half):
        pl.semaphore_signal(barrier, inc=1, device_id=device(ahead(0, kq), core), device_id_type=MESH)
    pl.semaphore_wait(barrier, grps + half - 1)

    def ag_z(src, buf, it, kz):
        return remote(src, buf.at[core, chip], agz_send.at[it, kz], agz_recv.at[it, kz], device(ahead(kz, 0), core))

    def ag_q(src, buf, it, kz, kq):
        return remote(
            src, buf.at[core, behind(kz, 0)], agq_send.at[it, kz, kq], agq_recv.at[it, kz, kq], device(ahead(0, kq), core)
        )

    def fw_copy(src, buf, it, kz, kq):
        return remote(src, buf.at[core, behind(kz, kq)], fw_send.at[it, kz, kq], fw_recv.at[it, kz, kq], partner)

    def spread(src, buf, it, kz):
        for kq in range(1, half):
            ag_q(src, buf, it, kz, kq).start()
        fw_copy(src, buf, it, kz, 0).start()

    def gather_start(src, buf, it):
        for kz in range(1, grps):
            ag_z(src, buf, it, kz).start()
        spread(src, buf, it, 0)

    def gather_spread(buf, it, kz):
        mine_now = buf.at[core, behind(kz, 0)]
        remote(
            mine_now, mine_now, agz_send.at[it, kz], agz_recv.at[it, kz], device(ahead(kz, 0), core)
        ).wait_recv()
        spread(mine_now, buf, it, kz)

    def gather_forward(buf, it, meet, acc):
        for kz in range(grps):
            for kq in range(1, half):
                j = behind(kz, kq)
                mine_now = buf.at[core, j]
                remote(
                    mine_now, mine_now, agq_send.at[it, kz, kq], agq_recv.at[it, kz, kq], device(ahead(0, kq), core)
                ).wait_recv()
                fw_copy(mine_now, buf, it, kz, kq).start()
                acc = meet(acc, core, j)
        return acc

    def gather_finish(src, buf, it, meet, acc):
        for kz in range(grps):
            for kq in range(half):
                j = behind(kz, kq)
                other_now = buf.at[1 - core, j]
                remote(other_now, other_now, fw_send.at[it, kz, kq], fw_recv.at[it, kz, kq], partner).wait_recv()
                acc = meet(acc, 1 - core, j)
        for kz in range(grps):
            held = src if kz == 0 else buf.at[core, behind(kz, 0)]
            if kz > 0:
                ag_z(src, buf, it, kz).wait_send()
            for kq in range(half):
                if kq > 0:
                    ag_q(held, buf, it, kz, kq).wait_send()
                fw_copy(held if kq == 0 else buf.at[core, behind(kz, kq)], buf, it, kz, kq).wait_send()
        return acc

    def block(buf, b):
        pieces = []
        for i in range(per):
            p = b * per + i
            pieces.append(buf[lax.rem(p, 2), p // 2])
        return pieces[0] if per == 1 else jnp.concatenate(pieces, axis=1)

    def apply(buf, parts):
        for t in range(nt):
            row = split(block(buf, list_ref[t, 0]))
            col = split(block(buf, list_ref[t, 1]))
            parts[2 * t] = fold(dot_nt(col, high[t]) + dot_nt(col, low[t]))
            parts[2 * t + 1] = fold(dot_nn(row, high[t]) + dot_nn(row, low[t]))

    def piece(p, parts):
        b = p // per
        at = pl.ds(pl.multiple_of(lax.rem(p, per) * width, width), width)
        zero = jnp.zeros((s, width), F32)
        acc = zero
        for t in range(nt):
            acc = acc + jnp.where(list_ref[t, 0] == b, parts[2 * t, :, at], zero)
            acc = acc + jnp.where(list_ref[t, 1] == b, parts[2 * t + 1, :, at], zero)
        return acc

    def ex_copy(other, it, j):
        return remote(away.at[j], other.at[j], ex_send.at[it, j], ex_recv.at[it, j], partner)

    def rsq_copy(came, it, kz, kq):
        return remote(
            mine.at[ahead(kz, kq)], came.at[kz, kq], rsq_send.at[it, kz, kq], rsq_recv.at[it, kz, kq],
            device(ahead(0, kq), core),
        )

    def rsz_copy(came, it, kz):
        return remote(
            mine.at[ahead(kz, 0)], came.at[kz, 0], rsz_send.at[it, kz], rsz_recv.at[it, kz],
            device(ahead(kz, 0), core),
        )

    zs = list(range(1, grps)) + [0]
    qs = list(range(1, half)) + [0]

    def scatter_start(other, came, it, parts):
        def order_of(i):
            return ahead(lax.rem(i // half + 1, grps), lax.rem(lax.rem(i, half) + 1, half))

        @pl.loop(0, chips)
        def _(i):
            j = order_of(i)
            away[j] = piece(2 * j + 1 - core, parts)
            ex_copy(other, it, j).start()

        @pl.loop(0, chips)
        def _(i):
            j = order_of(i)
            mine[j] = piece(2 * j + core, parts)

        for kz in zs:
            for kq in qs:
                j = ahead(kz, kq)
                ex_copy(other, it, j).wait_recv()
                mine[j] = mine[j] + other[j]
                if kq > 0:
                    rsq_copy(came, it, kz, kq).start()

    def scatter_columns(came, it):
        for kz in zs:
            j = ahead(kz, 0)
            acc = mine[j]
            for kq in range(1, half):
                rsq_copy(came, it, kz, kq).wait_recv()
                acc = acc + came[kz, kq]
            mine[j] = acc
            if kz > 0:
                rsz_copy(came, it, kz).start()

    def scatter_finish(came, it):
        total = mine[chip]
        for kz in range(1, grps):
            rsz_copy(came, it, kz).wait_recv()
            total = total + came[kz, 0]
        for kz in range(grps):
            if kz > 0:
                rsz_copy(came, it, kz).wait_send()
            for kq in range(half):
                if kq > 0:
                    rsq_copy(came, it, kz, kq).wait_send()
                ex_copy(other0, it, ahead(kz, kq)).wait_send()
        return total

    def gram_all(first, second):
        def step(j, acc):
            for c in range(2):
                acc = acc + gram_small(first[c, j], second[c, j])
            return acc

        return lax.fori_loop(0, chips, step, jnp.zeros((s, s), F32), unroll=4)

    gather_start(rhs_ref, field, 0)
    field[core, chip] = rhs_ref[...]

    chunk = min(128, order)

    def prepare(t):
        loads(t).wait()
        differ = list_ref[t, 0] != list_ref[t, 1]

        @pl.loop(0, order // chunk)
        def _(i):
            at = pl.ds(pl.multiple_of(i * chunk, chunk), chunk)
            x = stage[t, at, :]
            rows = lax.broadcasted_iota(jnp.int32, x.shape, 0) + i * chunk
            cols = lax.broadcasted_iota(jnp.int32, x.shape, 1)
            weight = jnp.where(rows > cols, 1.0, jnp.where(rows == cols, 0.5, 0.0))
            weight = jnp.where(differ, 1.0, weight)
            x = x * weight
            hi = x.astype(BF16)
            high[t, at, :] = hi
            low[t, at, :] = (x - hi.astype(F32)).astype(BF16)

    for i in range(max(nt, grps - 1)):
        if i < nt:
            prepare(i)
        if i + 1 < grps:
            gather_spread(field, 0, i + 1)
    def nothing(acc, c, j):
        return acc

    gather_forward(field, 0, nothing, None)
    gather_finish(rhs_ref, field, 0, nothing, None)

    apply(field, parts0)
    scatter_start(other0, came0, 0, parts0)
    norm0 = gram_all(field, field)
    scatter_columns(came0, 0)
    own_rhs = rhs_ref[...]
    own_ridge = ridge_ref[...]
    own_image = scatter_finish(came0, 0) + own_ridge * own_rhs
    image[core, chip] = own_image
    gather_start(image.at[core, chip], image, 1)

    def meet(acc, c, j):
        return acc + gram_small(field[c, j], image[c, j])

    pq = gram_small(own_rhs, own_image)
    for kz in range(1, grps):
        gather_spread(image, 1, kz)
        pq = meet(pq, core, behind(kz, 0))
    pq = gather_forward(image, 1, meet, pq)
    pq = gather_finish(image.at[core, chip], image, 1, meet, pq)

    apply(image, parts1)
    scatter_start(other1, came1, 1, parts1)
    alpha = gauss_solve(pq, norm0)
    alpha_t = mixer(alpha.T)

    def residual_step(j, acc):
        for c in range(2):
            r = field[c, j] - mixed(alpha_t, image[c, j])
            acc = acc + gram_small(r, r)
        return acc

    norm1 = lax.fori_loop(0, chips, residual_step, jnp.zeros((s, s), F32), unroll=4)
    beta = gauss_solve(norm0, norm1)
    beta_t = mixer(beta.T)

    def onward(first, second):
        return (first - mixed(alpha_t, second)) + mixed(beta_t, first)

    own_res = own_rhs - mixed(alpha_t, own_image)
    own_dir = own_res + mixed(beta_t, own_rhs)
    partial = gram_small(own_dir, own_dir * own_ridge)
    for t in range(nt):
        b = list_ref[t, 0]
        g = gram_small(onward(block(field, b), block(image, b)), onward(parts0[2 * t], parts1[2 * t]))
        partial = partial + g + g.T
    pad = jnp.concatenate([partial, jnp.zeros((s, 128 - s), F32)], axis=1)
    small[...] = pad
    sm_ex = remote(small, small_other, sm_send.at[0], sm_recv.at[0], partner)
    sm_ex.start()
    scatter_columns(came1, 1)
    sm_ex.wait_recv()
    small_sum[0] = pad + small_other[...]

    def smq_copy(kq):
        return remote(
            small_sum.at[0], small_in.at[0, kq], smq_send.at[kq], smq_recv.at[kq], device(ahead(0, kq), core)
        )

    def smz_copy(kz):
        return remote(
            small_sum.at[1], small_in.at[1, kz], smz_send.at[kz], smz_recv.at[kz], device(ahead(kz, 0), core)
        )

    for kq in range(1, half):
        smq_copy(kq).start()
    acc = small_sum[0]
    for kq in range(1, half):
        smq_copy(kq).wait_recv()
        acc = acc + small_in[0, kq]
    small_sum[1] = acc
    for kz in range(1, grps):
        smz_copy(kz).start()
    sol_ref[...] = mixed(alpha_t, own_rhs)
    for kz in range(1, grps):
        smz_copy(kz).wait_recv()
        acc = acc + small_in[1, kz]
    alpha1_t = mixer(gauss_solve(acc[:, :s], norm1).T)
    sol_ref[...] = sol_ref[...] + mixed(alpha1_t, own_dir)
    spread_image = scatter_finish(came1, 1) + own_ridge * own_image
    res_ref[...] = own_res - mixed(alpha1_t, onward(own_image, spread_image))

    for kq in range(1, half):
        smq_copy(kq).wait_send()
    for kz in range(1, grps):
        smz_copy(kz).wait_send()
    sm_ex.wait_send()


def solution(mesh):
    grps, tiles_axis = mesh.shape["grp"], mesh.shape["tile"]
    half = tiles_axis // 2
    chips = grps * half

    def local(right_side, ridge, tiles, tile_list):
        s, width = right_side.shape
        nt, order = tiles.shape[0], tiles.shape[1]
        vmem = pl.BlockSpec(memory_space=pltpu.VMEM)
        out = jax.ShapeDtypeStruct((s, width), F32)
        dma = pltpu.SemaphoreType.DMA
        return pl.pallas_call(
            functools.partial(kernel, grps, tiles_axis),
            out_shape=(out, out),
            in_specs=[
                pl.BlockSpec(memory_space=pltpu.SMEM),
                vmem,
                vmem,
                pl.BlockSpec(memory_space=pl.ANY),
            ],
            out_specs=(vmem, vmem),
            scratch_shapes=[
                pltpu.VMEM((nt, order, order), F32),
                pltpu.VMEM((nt, order, order), BF16),
                pltpu.VMEM((nt, order, order), BF16),
                pltpu.VMEM((2, chips, s, width), F32),
                pltpu.VMEM((2, chips, s, width), F32),
                pltpu.VMEM((2 * nt, s, order), F32),
                pltpu.VMEM((2 * nt, s, order), F32),
                pltpu.VMEM((chips, s, width), F32),
                pltpu.VMEM((chips, s, width), F32),
                pltpu.VMEM((chips, s, width), F32),
                pltpu.VMEM((chips, s, width), F32),
                pltpu.VMEM((grps, half, s, width), F32),
                pltpu.VMEM((grps, half, s, width), F32),
                pltpu.VMEM((s, 128), F32),
                pltpu.VMEM((2, s, 128), F32),
                pltpu.VMEM((2, max(half, grps), s, 128), F32),
                pltpu.VMEM((s, 128), F32),
                dma((nt,)),
                dma((2, grps)),
                dma((2, grps)),
                dma((2, grps, half)),
                dma((2, grps, half)),
                dma((2, grps, half)),
                dma((2, grps, half)),
                dma((2, chips)),
                dma((2, chips)),
                dma((2, grps)),
                dma((2, grps)),
                dma((2, grps, half)),
                dma((2, grps, half)),
                dma((1,)),
                dma((1,)),
                dma((half,)),
                dma((half,)),
                dma((grps,)),
                dma((grps,)),
            ],
            compiler_params=pltpu.CompilerParams(
                collective_id=0, has_side_effects=True, vmem_limit_bytes=60 * 1024 * 1024
            ),
        )(tile_list, right_side, ridge[None, :], tiles)

    return jax.shard_map(
        local,
        mesh=mesh,
        in_specs=(
            P(None, ("grp", "tile")),
            P(("grp", "tile")),
            P(("grp", "tile"), None, None),
            P(("grp", "tile"), None),
        ),
        out_specs=(P(None, ("grp", "tile")), P(None, ("grp", "tile"))),
        check_vma=False,
    )
```
